32 devices in a mesh: groups: 2 (over y), ctx: 4 (over z), heads: 2 (over x), rep: 2 (over core).
Axes of the slice: x: 2, y: 2, z: 4, core: 2. Of those that a mesh axis runs over, the one named last changes fastest.
Arguments:
- queries: bfloat16 [256, 128, 128], P(('groups', 'ctx', 'rep'), 'heads'), parts along dimension 0, may hold values from -10 to 10
- cache_keys: bfloat16 [16384, 8, 128], P(('groups', 'ctx'), 'heads'), parts along dimension 0, may hold values from -10 to 10
- cache_values: bfloat16 [16384, 8, 128], P(('groups', 'ctx'), 'heads'), parts along dimension 0, may hold values from -6 to 6
- new_keys: bfloat16 [256, 8, 128], P(('groups', 'ctx', 'rep'), 'heads'), parts along dimension 0, may hold values from -6 to 6
- new_values: bfloat16 [256, 8, 128], P(('groups', 'ctx', 'rep'), 'heads'), parts along dimension 0, may hold values from -6 to 6
- positions: int32 [256], P(('groups', 'ctx', 'rep')), parts along dimension 0, may hold values from 2 to 8191
- cached_length: int32 [2], P('groups'), parts along dimension 0, may hold values from 4096 to 8192
- out_weight: bfloat16 [16384, 16384], P('heads', ('ctx', 'rep')), may hold values from -0.046875 to 0.046875
Outputs:
- mixed: bfloat16 [256, 16384], P(('groups', 'heads'), ('ctx', 'rep')), parts along dimension 0
The draws below stay inside these ranges and needn't reach their ends.
There are 2 independent parts, one for each index of `groups`. The reference program is written for one: setup_inputs(seed, part) draws one part's arguments, and reference() takes and returns one part's arrays. A program takes and returns all parts, laid end to end along the dimension named above; an argument that names none is the same for every part. Nothing has to cross between parts.
All inputs are finite; a program needn't handle non-finite values.
Results may differ from the reference program's by a relative error of at most 0.0052.
Values may be sent and summed in bfloat16 or wider, within the bound.
No kernel may reach another device: no remote copies, remote signals or barrier semaphores. Data moves between devices by JAX's collectives and lax.ppermute only.
A program may use at most 128 MiB of HBM per device.

```python
import jax
import jax.numpy as jnp
from jax import lax

D = 16384
H = 128
KVH = 8
HD = 128
KV_DEV = 2048
NQ = 128
CTX = 8192
N_CTX = 4


def draw_queries(key, part):
    base = jnp.clip(jax.random.normal(jax.random.fold_in(key, 1), (NQ, H, HD), jnp.float32), -6.0, 6.0)
    return base.astype(jnp.bfloat16)


def draw_cache_keys(key, part):
    base = jnp.clip(jax.random.normal(jax.random.fold_in(key, 3), (CTX, KVH, HD), jnp.float32), -6.0, 6.0)
    return base.astype(jnp.bfloat16)


def plant(drawn, own_key, least, largest):
    index_at = [jax.random.randint(jax.random.fold_in(own_key, axis), (), 0, length) for axis, length in enumerate(drawn.shape)]
    widest = drawn.shape.index(max(drawn.shape))
    neighbour = index_at[:widest] + [(index_at[widest] + 1) % drawn.shape[widest]] + index_at[widest + 1:]
    return drawn.at[tuple(index_at)].set(least).at[tuple(neighbour)].set(largest)


def block_levels(own_key, dims, split, low, largest):
    factor_of = 1.0
    for dim, parts in split:
        heights = jax.random.uniform(jax.random.fold_in(jax.random.fold_in(own_key, 6), dim), (parts,), jnp.float32, low / len(split), largest / len(split))
        factor_of = factor_of * jnp.repeat(jnp.exp(heights), dims[dim] // parts).reshape((-1,) + (1,) * (len(dims) - 1 - dim))
    return factor_of


def normal_values(key, shape, scale, most, pieces=(), held_as=jnp.bfloat16):
    entries = jax.random.normal(key, shape, jnp.float32) * scale
    if len(pieces) > 0:
        entries = block_levels(key, shape, pieces, -0.22, 0.18) * entries
    return jnp.clip(entries, min=-most, max=most).astype(held_as)


def setup_inputs(seed: int = 0, part: int = 0) -> dict:
    key_of = jax.random.split(jax.random.key(seed), 9)
    own_keys = jax.random.split(jax.random.fold_in(key_of[8], part), 9)
    return {
        "queries": draw_queries(jax.random.fold_in(jax.random.fold_in(key_of[8], part), 71), part),
        "cache_keys": draw_cache_keys(jax.random.fold_in(jax.random.fold_in(key_of[8], part), 71), part),
        "cache_values": normal_values(own_keys[2], (CTX, KVH, HD), 1.0, 6.0, ((0, 4), (1, 2))),
        "new_keys": normal_values(own_keys[3], (NQ, KVH, HD), 1.0, 6.0, ((0, 8), (1, 2))),
        "new_values": normal_values(own_keys[4], (NQ, KVH, HD), 1.0, 6.0, ((0, 8), (1, 2))),
        "positions": plant(jax.random.randint(own_keys[5], (NQ,), 2, CTX), jax.random.fold_in(own_keys[5], 1), 2, CTX - 1).astype(jnp.int32),
        "cached_length": jax.random.randint(own_keys[6], (1,), CTX // 2, CTX + 1).astype(jnp.int32),
        "out_weight": normal_values(key_of[7], (H * HD, D), (H * HD) ** -0.5, 0.046875, ((0, 2), (1, 8))),
    }


NEG_FILL = -1e30


def combine(state, update):
    maxima, totals, values = state
    new_max, new_tot, new_val = update
    highest = jnp.maximum(maxima, new_max)
    keeping = jnp.exp(maxima - highest)
    taking = jnp.exp(new_max - highest)
    return highest, keeping * totals + taking * new_tot, keeping[..., None] * values + taking[..., None] * new_val


def reference(queries, cache_keys, cache_values, new_keys, new_values, positions, cached_length, out_weight):
    per_group = H // KVH
    scale_factor = HD ** -0.5
    limits = jnp.minimum(cached_length[0], positions).astype(jnp.int32)
    grouped = queries.astype(jnp.float32).reshape(NQ, KVH, per_group, HD)
    own_score = jnp.einsum('tkgd,tkd->tkg', grouped, new_keys.astype(jnp.float32), precision=lax.Precision.HIGHEST) * scale_factor
    own_values = jnp.broadcast_to(new_values.astype(jnp.float32)[:, :, None, :], (NQ, KVH, per_group, HD)).reshape(NQ, H, HD)
    start_state = (own_score.reshape(NQ, H), jnp.ones((NQ, H), jnp.float32), own_values)
    key_blocks = cache_keys.reshape(N_CTX, KV_DEV, KVH, HD)
    value_blocks = cache_values.reshape(N_CTX, KV_DEV, KVH, HD)

    def visit(state, inputs):
        block_keys, block_values, index = inputs
        scores = jnp.einsum('tkgd,jkd->tkgj', grouped, block_keys.astype(jnp.float32), precision=lax.Precision.HIGHEST) * scale_factor
        slots = index * KV_DEV + jnp.arange(KV_DEV, dtype=jnp.int32)
        visible = (slots[None, :] < limits[:, None])[:, None, None, :]
        scores = jnp.where(visible, scores, NEG_FILL)
        maxima = jnp.max(scores, axis=-1)
        weights = jnp.where(visible, jnp.exp(scores - maxima[..., None]), 0.0)
        totals = jnp.sum(weights, axis=-1)
        rounded = lax.optimization_barrier(weights.astype(jnp.bfloat16))
        output = jnp.einsum('tkgj,jkd->tkgd', rounded.astype(jnp.float32), block_values.astype(jnp.float32), precision=lax.Precision.HIGHEST)
        update = (maxima.reshape(NQ, H), totals.reshape(NQ, H), output.reshape(NQ, H, HD))
        return combine(state, update), None

    final, _ = lax.scan(visit, start_state, (key_blocks, value_blocks, jnp.arange(N_CTX, dtype=jnp.int32)))
    attended = (final[2] / final[1][..., None]).astype(jnp.bfloat16).reshape(NQ, H * HD)
    return jnp.dot(attended, out_weight, preferred_element_type=jnp.float32).astype(jnp.bfloat16)
```

```python
import functools
import math

import jax
import jax.numpy as jnp
from jax import lax
from jax.experimental import pallas as pl
from jax.experimental.pallas import tpu as pltpu
from jax.sharding import PartitionSpec as P

NEG_FILL = -1e30
NEG_FLOOR = -1e29
LANES = 128
PACK = 16
VMEM = pltpu.MemorySpace.VMEM
SMEM = pltpu.MemorySpace.SMEM


def round_up(value, step):
    return (value + step - 1) // step * step


def stat_rows(rows):
    return round_up(3 * (rows // LANES), PACK)


def attend_kernel(
    tokens, kv_heads, per_group, with_own, base_ref, q_ref, k_ref, v_ref, *rest
):
    if with_own:
        nk_ref, nv_ref, out_ref, bound_ref = rest
    else:
        out_ref, bound_ref = rest
    head_rows = tokens * per_group
    rows = kv_heads * head_rows
    block_len, size = k_ref.shape[1:]
    factor = size ** (-0.5) * math.log2(math.e)
    high = q_ref[rows : rows + tokens, :].astype(jnp.float32)
    low = q_ref[rows + tokens : rows + 2 * tokens, :].astype(jnp.float32)
    bound = high * 128.0 + low - base_ref[0].astype(jnp.float32)
    bound_ref[...] = jnp.broadcast_to(bound[:, None, :], (tokens, per_group, LANES)).reshape(
        head_rows, LANES
    )
    lane = lax.broadcasted_iota(jnp.int32, (1, LANES), 1).astype(jnp.float32)
    lane_id = lax.broadcasted_iota(jnp.int32, (LANES, LANES), 1)
    stats = jnp.zeros((LANES, LANES), jnp.float32)
    limit = bound_ref[...]
    for head in range(kv_heads):
        q = q_ref[head * head_rows : (head + 1) * head_rows, :]
        scores = lax.dot_general(
            q, k_ref[head], (((1,), (1,)), ((), ())), preferred_element_type=jnp.float32
        )
        pieces = []
        for start in range(0, block_len, LANES):
            seen = (lane + float(start)) < limit
            pieces.append(jnp.where(seen, scores[:, start : start + LANES], NEG_FILL))
        best = functools.reduce(jnp.maximum, pieces)
        top = jnp.max(best, axis=-1, keepdims=True)
        if with_own:
            nk = jnp.broadcast_to(
                nk_ref[head].astype(jnp.float32)[:, None, :], (tokens, per_group, size)
            ).reshape(head_rows, size)
            own = jnp.sum(q.astype(jnp.float32) * nk, axis=-1, keepdims=True)
            top = jnp.maximum(top, own)
        top = jnp.maximum(top, NEG_FLOOR)
        weights = [jnp.exp2((piece - top) * factor) for piece in pieces]
        total = jnp.sum(functools.reduce(jnp.add, weights), axis=-1, keepdims=True)
        rounded = jnp.concatenate([w.astype(jnp.bfloat16) for w in weights], axis=1)
        value = lax.dot_general(
            rounded, v_ref[head], (((1,), (0,)), ((), ())), preferred_element_type=jnp.float32
        )
        if with_own:
            nv = jnp.broadcast_to(
                nv_ref[head].astype(jnp.float32)[:, None, :], (tokens, per_group, size)
            ).reshape(head_rows, size)
            mine = jnp.exp2((own - top) * factor)
            total = total + mine
            value = value + mine * nv
        some = total > 0.0
        safe = jnp.where(some, total, 1.0)
        out_ref[head * head_rows : (head + 1) * head_rows, :] = (value / safe).astype(jnp.bfloat16)
        level = jnp.where(some, top * factor + jnp.log2(safe), NEG_FILL)
        for part in range(head_rows // LANES):
            column = level[part * LANES : (part + 1) * LANES, :]
            index = head * (head_rows // LANES) + part
            stats = jnp.where(lane_id == index, column, stats)
    flat = jnp.transpose(stats)
    first = flat.astype(jnp.bfloat16)
    rest_one = flat - first.astype(jnp.float32)
    second = rest_one.astype(jnp.bfloat16)
    third = (rest_one - second.astype(jnp.float32)).astype(jnp.bfloat16)
    count = rows // LANES
    extra = stat_rows(rows)
    joined = jnp.concatenate(
        [
            first.astype(jnp.float32)[:count],
            second.astype(jnp.float32)[:count],
            third.astype(jnp.float32)[:count],
            jnp.zeros((extra - 3 * count, LANES), jnp.float32),
        ],
        axis=0,
    )
    out_ref[rows : rows + extra, :] = joined.astype(jnp.bfloat16)


def attend(base, packed, keys, values, own, tokens, per_group):
    kv_heads, block_len, size = keys.shape
    rows = tokens * kv_heads * per_group
    body = functools.partial(attend_kernel, tokens, kv_heads, per_group, own is not None)
    spec = pl.BlockSpec(memory_space=VMEM)
    operands = (base, packed, keys, values) + (own if own is not None else ())
    return pl.pallas_call(
        body,
        out_shape=jax.ShapeDtypeStruct((rows + stat_rows(rows), size), jnp.bfloat16),
        in_specs=[pl.BlockSpec(memory_space=SMEM)] + [spec] * (len(operands) - 1),
        out_specs=spec,
        scratch_shapes=[pltpu.VMEM((tokens * per_group, LANES), jnp.float32)],
        compiler_params=pltpu.CompilerParams(vmem_limit_bytes=24 * 1024 * 1024),
        cost_estimate=pl.CostEstimate(
            flops=4 * rows * block_len * size,
            bytes_accessed=4 * kv_heads * block_len * size,
            transcendentals=rows * block_len,
        ),
        name="attend",
    )(*operands)


def merge_kernel(tokens, kv_heads, per_group, count, *refs):
    parts, out_ref, hold_ref = refs[:count], refs[count], refs[count + 1]
    head_rows = tokens * per_group
    rows = kv_heads * head_rows
    lines = rows // LANES
    levels = []
    for part in parts:
        tail = part[rows:, :].astype(jnp.float32)
        levels.append(tail[:lines] + tail[lines : 2 * lines] + tail[2 * lines : 3 * lines])
    top = functools.reduce(jnp.maximum, levels)
    shares = [jnp.exp2(level - top) for level in levels]
    whole = functools.reduce(jnp.add, shares)
    shares = [share / whole for share in shares]
    stacked = jnp.concatenate(
        shares + [jnp.zeros((LANES - count * lines, LANES), jnp.float32)], axis=0
    )
    columns = jnp.transpose(stacked)
    for head in range(kv_heads):
        for piece in range(head_rows // LANES):
            line = head * (head_rows // LANES) + piece
            start = line * LANES
            value = None
            for index, part in enumerate(parts):
                share = columns[:, index * lines + line : index * lines + line + 1]
                term = share * part[start : start + LANES, :].astype(jnp.float32)
                value = term if value is None else value + term
            hold_ref[piece * LANES : (piece + 1) * LANES, :] = value
        for member in range(per_group):
            column = (head * per_group + member) * LANES
            out_ref[:, column : column + LANES] = hold_ref[
                pl.ds(member, tokens, stride=per_group), :
            ].astype(jnp.bfloat16)


def merge(parts, tokens, kv_heads, per_group):
    rows = tokens * kv_heads * per_group
    spec = pl.BlockSpec(memory_space=VMEM)
    return pl.pallas_call(
        functools.partial(merge_kernel, tokens, kv_heads, per_group, len(parts)),
        out_shape=jax.ShapeDtypeStruct((tokens, kv_heads * per_group * LANES), jnp.bfloat16),
        in_specs=[spec] * len(parts),
        out_specs=spec,
        scratch_shapes=[pltpu.VMEM((tokens * per_group, LANES), jnp.float32)],
        compiler_params=pltpu.CompilerParams(vmem_limit_bytes=8 * 1024 * 1024),
        cost_estimate=pl.CostEstimate(
            flops=4 * len(parts) * rows * LANES,
            bytes_accessed=2 * len(parts) * rows * LANES,
            transcendentals=0,
        ),
        name="merge",
    )(*parts)


def project_kernel(count, near, place_ref, *refs):
    blocks, w_ref, near_ref, far_ref, left_ref = (
        refs[:count],
        refs[count],
        refs[count + 1],
        refs[count + 2],
        refs[count + 3],
    )

    @pl.when(pl.program_id(0) == 0)
    def _():
        for index, block in enumerate(blocks):
            tokens = block.shape[0]
            start = pl.multiple_of(place_ref[index], tokens)
            left_ref[pl.ds(start, tokens), :] = block[...]

    result = jnp.dot(left_ref[...], w_ref[...], preferred_element_type=jnp.float32)
    near_ref[...] = result[:near]
    far_ref[...] = result[near:].astype(jnp.bfloat16)


def project(places, blocks, weight, near, tile):
    depth, width = weight.shape
    total = sum(block.shape[0] for block in blocks)
    whole = [pl.BlockSpec(block.shape, lambda j: (0, 0)) for block in blocks]
    return pl.pallas_call(
        functools.partial(project_kernel, len(blocks), near),
        out_shape=(
            jax.ShapeDtypeStruct((near, width), jnp.float32),
            jax.ShapeDtypeStruct((total - near, width), jnp.bfloat16),
        ),
        grid=(width // tile,),
        in_specs=[pl.BlockSpec(memory_space=SMEM)]
        + whole
        + [pl.BlockSpec((depth, tile), lambda j: (0, j))],
        out_specs=(
            pl.BlockSpec((near, tile), lambda j: (0, j)),
            pl.BlockSpec((total - near, tile), lambda j: (0, j)),
        ),
        scratch_shapes=[pltpu.VMEM((total, depth), jnp.bfloat16)],
        compiler_params=pltpu.CompilerParams(vmem_limit_bytes=28 * 1024 * 1024),
        cost_estimate=pl.CostEstimate(
            flops=2 * total * depth * width,
            bytes_accessed=2 * depth * width,
            transcendentals=0,
        ),
        name="project",
    )(places, *blocks, weight)


def split_index(index, pair):
    return index // pair, index % pair


def ctx_routes(count):
    pair = 2 if count % 2 == 0 else 1
    return pair, count // pair


def moved(value, count, step, flip):
    pair, spans = ctx_routes(count)
    pairs = []
    for source in range(count):
        span, side = split_index(source, pair)
        pairs.append((source, ((span + step) % spans) * pair + (side + flip) % pair))
    return lax.ppermute(value, "ctx", pairs)


def gather_blocks(value, count):
    pair, spans = ctx_routes(count)
    blocks = [((0, 0), value)]
    if pair > 1:
        blocks.append(((0, 1), moved(value, count, 0, 1)))
    for step in range(1, spans):
        crossed = moved(value, count, -step, 0)
        blocks.append(((step, 0), crossed))
    for key, crossed in list(blocks):
        if pair > 1 and key[0] > 0:
            blocks.append(((key[0], 1), moved(crossed, count, 0, 1)))
    return blocks


def local(
    queries, cache_keys, cache_values, new_keys, new_values, positions, cached_length, out_weight
):
    tokens, local_heads, size = queries.shape
    block_len, kv_heads = cache_keys.shape[0], cache_keys.shape[1]
    per_group = local_heads // kv_heads
    n_ctx = lax.axis_size("ctx")
    n_rep = lax.axis_size("rep")
    n_heads = lax.axis_size("heads")
    ctx = lax.axis_index("ctx")
    rep = lax.axis_index("rep")
    side = lax.axis_index("heads")
    pair, spans = ctx_routes(n_ctx)
    base = (ctx * block_len).astype(jnp.int32).reshape(1)

    limits = jnp.minimum(cached_length[0], positions)
    marks = jnp.concatenate([limits // 128, limits % 128]).astype(jnp.bfloat16)
    marks = jnp.broadcast_to(marks[:, None], (2 * tokens, size))
    ordered = queries.reshape(tokens, kv_heads, per_group, size).transpose(1, 0, 2, 3)
    packed = jnp.concatenate([ordered.reshape(tokens * local_heads, size), marks], axis=0)

    keys = cache_keys.transpose(1, 0, 2)
    values = cache_values.transpose(1, 0, 2)
    own = (new_keys.transpose(1, 0, 2), new_values.transpose(1, 0, 2))

    parts = []
    for (step, flip), block in gather_blocks(packed, n_ctx):
        home = step == 0 and flip == 0
        part = attend(base, block, keys, values, own if home else None, tokens, per_group)
        parts.append(part if home else moved(part, n_ctx, step, flip))
    attended = merge(parts, tokens, kv_heads, per_group)

    group_tokens = n_ctx * n_rep * tokens
    near = group_tokens // n_heads
    span, which = ctx // pair, ctx % pair
    blocks, places = [], []
    for (step, flip), block in gather_blocks(attended, n_ctx):
        source = ((span + step) % spans) * pair + (which + flip) % pair
        for turn in range(n_rep):
            passed = block
            if turn:
                passed = lax.ppermute(
                    block, "rep", [(i, (i - turn) % n_rep) for i in range(n_rep)]
                )
            row = (source * n_rep + (rep + turn) % n_rep) * tokens
            places.append((row - side * near) % group_tokens)
            blocks.append(passed)
    places = jnp.stack(places).astype(jnp.int32)
    width = out_weight.shape[1]
    mine, others = project(places, blocks, out_weight, near, min(256, width))
    result = mine
    for step in range(1, n_heads):
        sent = others[(step - 1) * near : step * near]
        result = result + lax.ppermute(
            sent, "heads", [(i, (i + step) % n_heads) for i in range(n_heads)]
        ).astype(jnp.float32)
    return result.astype(jnp.bfloat16)


def solution(mesh):
    return jax.shard_map(
        local,
        mesh=mesh,
        in_specs=(
            P(("groups", "ctx", "rep"), "heads", None),
            P(("groups", "ctx"), "heads", None),
            P(("groups", "ctx"), "heads", None),
            P(("groups", "ctx", "rep"), "heads", None),
            P(("groups", "ctx", "rep"), "heads", None),
            P(("groups", "ctx", "rep")),
            P("groups"),
            P("heads", ("ctx", "rep")),
        ),
        out_specs=P(("groups", "heads"), ("ctx", "rep")),
        check_vma=False,
    )
```

```python
import functools
import math

import jax
import jax.numpy as jnp
from jax import lax
from jax.experimental import pallas as pl
from jax.experimental.pallas import tpu as pltpu
from jax.sharding import PartitionSpec as P

NEG_FILL = -1e30
NEG_FLOOR = -1e29
LANES = 128
PACK = 16
VMEM = pltpu.MemorySpace.VMEM


def round_up(value, step):
    return (value + step - 1) // step * step


def stat_rows(rows):
    return round_up(3 * (rows // LANES), PACK)


def attend_kernel(
    tokens, heads, per_group, with_own, load_rows, q_ref, k_ref, v_ref, *rest
):
    rest = list(rest)
    if with_own:
        nk_ref, nv_ref = rest.pop(0), rest.pop(0)
    if load_rows is not None:
        w_ref = rest.pop(0)
    out_ref = rest.pop(0)
    copy = None
    if load_rows is not None:
        copy = pltpu.make_async_copy(
            w_ref.at[load_rows[0] : load_rows[1], :], rest.pop(0), rest.pop()
        )
        copy.start()
    bound_ref = rest.pop(0)
    head_rows = tokens * per_group
    kv_heads, block_len, size = k_ref.shape
    rows = len(heads) * head_rows
    local_heads = kv_heads * per_group
    factor = size ** (-0.5) * math.log2(math.e)
    high = q_ref[tokens * local_heads : tokens * local_heads + tokens, :].astype(jnp.float32)
    low = q_ref[tokens * local_heads + tokens :, :].astype(jnp.float32)
    base = lax.axis_index("ctx").astype(jnp.int32) * block_len
    bound = high * 128.0 + low - base.astype(jnp.float32)
    bound_ref[...] = jnp.broadcast_to(bound[:, None, :], (tokens, per_group, LANES)).reshape(
        head_rows, LANES
    )
    lane = lax.broadcasted_iota(jnp.int32, (1, LANES), 1).astype(jnp.float32)
    lane_id = lax.broadcasted_iota(jnp.int32, (LANES, LANES), 1)
    stats = jnp.zeros((LANES, LANES), jnp.float32)
    limit = bound_ref[...]
    for order, head in enumerate(heads):
        q = jnp.concatenate(
            [
                q_ref[t * local_heads + head * per_group : t * local_heads + (head + 1) * per_group, :]
                for t in range(tokens)
            ],
            axis=0,
        )
        scores = lax.dot_general(
            q, k_ref[head], (((1,), (1,)), ((), ())), preferred_element_type=jnp.float32
        )
        pieces = []
        for start in range(0, block_len, LANES):
            seen = (lane + float(start)) < limit
            pieces.append(jnp.where(seen, scores[:, start : start + LANES], NEG_FILL))
        best = functools.reduce(jnp.maximum, pieces)
        top = jnp.max(best, axis=-1, keepdims=True)
        if with_own:
            nk = jnp.broadcast_to(
                nk_ref[head].astype(jnp.float32)[:, None, :], (tokens, per_group, size)
            ).reshape(head_rows, size)
            own = jnp.sum(q.astype(jnp.float32) * nk, axis=-1, keepdims=True)
            top = jnp.maximum(top, own)
        top = jnp.maximum(top, NEG_FLOOR)
        weights = [jnp.exp2((piece - top) * factor) for piece in pieces]
        total = jnp.sum(functools.reduce(jnp.add, weights), axis=-1, keepdims=True)
        rounded = jnp.concatenate([w.astype(jnp.bfloat16) for w in weights], axis=1)
        value = lax.dot_general(
            rounded, v_ref[head], (((1,), (0,)), ((), ())), preferred_element_type=jnp.float32
        )
        if with_own:
            nv = jnp.broadcast_to(
                nv_ref[head].astype(jnp.float32)[:, None, :], (tokens, per_group, size)
            ).reshape(head_rows, size)
            mine = jnp.exp2((own - top) * factor)
            total = total + mine
            value = value + mine * nv
        some = total > 0.0
        safe = jnp.where(some, total, 1.0)
        out_ref[order * head_rows : (order + 1) * head_rows, :] = (value / safe).astype(jnp.bfloat16)
        level = jnp.where(some, top * factor + jnp.log2(safe), NEG_FILL)
        for part in range(head_rows // LANES):
            column = level[part * LANES : (part + 1) * LANES, :]
            index = order * (head_rows // LANES) + part
            stats = jnp.where(lane_id == index, column, stats)
    flat = jnp.transpose(stats)
    first = flat.astype(jnp.bfloat16)
    rest_one = flat - first.astype(jnp.float32)
    second = rest_one.astype(jnp.bfloat16)
    third = (rest_one - second.astype(jnp.float32)).astype(jnp.bfloat16)
    count = rows // LANES
    extra = stat_rows(rows)
    joined = jnp.concatenate(
        [
            first.astype(jnp.float32)[:count],
            second.astype(jnp.float32)[:count],
            third.astype(jnp.float32)[:count],
            jnp.zeros((extra - 3 * count, LANES), jnp.float32),
        ],
        axis=0,
    )
    out_ref[rows : rows + extra, :] = joined.astype(jnp.bfloat16)
    if copy is not None:
        copy.wait()


def attend(packed, keys, values, own, weight, load_rows, tokens, per_group, heads):
    kv_heads, block_len, size = keys.shape
    rows = tokens * len(heads) * per_group
    body = functools.partial(
        attend_kernel, tokens, heads, per_group, own is not None, load_rows
    )
    spec = pl.BlockSpec(memory_space=VMEM)
    operands = (packed, keys, values) + (own if own is not None else ())
    in_specs = [spec] * len(operands)
    shapes = [jax.ShapeDtypeStruct((rows + stat_rows(rows), size), jnp.bfloat16)]
    scratch = [pltpu.VMEM((tokens * per_group, LANES), jnp.float32)]
    if load_rows is not None:
        operands += (pltpu.with_memory_space_constraint(weight, pltpu.MemorySpace.HBM),)
        in_specs.append(pl.BlockSpec(memory_space=pltpu.MemorySpace.HBM))
        shapes.append(
            jax.ShapeDtypeStruct((load_rows[1] - load_rows[0], weight.shape[1]), weight.dtype)
        )
        scratch.append(pltpu.SemaphoreType.DMA)
    return pl.pallas_call(
        body,
        out_shape=shapes,
        in_specs=in_specs,
        out_specs=[spec] * len(shapes),
        scratch_shapes=scratch,
        compiler_params=pltpu.CompilerParams(vmem_limit_bytes=12 * 1024 * 1024),
        cost_estimate=pl.CostEstimate(
            flops=4 * rows * block_len * size,
            bytes_accessed=4 * len(heads) * block_len * size,
            transcendentals=rows * block_len,
        ),
        name="attend",
    )(*operands)


def merge_kernel(tokens, kv_heads, per_group, count, *refs):
    parts, out_ref, hold_ref = refs[:count], refs[count], refs[count + 1]
    head_rows = tokens * per_group
    rows = kv_heads * head_rows
    lines = rows // LANES
    levels = []
    for part in parts:
        tail = part[rows:, :].astype(jnp.float32)
        levels.append(tail[:lines] + tail[lines : 2 * lines] + tail[2 * lines : 3 * lines])
    top = functools.reduce(jnp.maximum, levels)
    shares = [jnp.exp2(level - top) for level in levels]
    whole = functools.reduce(jnp.add, shares)
    shares = [share / whole for share in shares]
    stacked = jnp.concatenate(
        shares + [jnp.zeros((LANES - count * lines, LANES), jnp.float32)], axis=0
    )
    columns = jnp.transpose(stacked)
    for head in range(kv_heads):
        for piece in range(head_rows // LANES):
            line = head * (head_rows // LANES) + piece
            start = line * LANES
            value = None
            for index, part in enumerate(parts):
                share = columns[:, index * lines + line : index * lines + line + 1]
                term = share * part[start : start + LANES, :].astype(jnp.float32)
                value = term if value is None else value + term
            hold_ref[piece * LANES : (piece + 1) * LANES, :] = value
        for member in range(per_group):
            column = (head * per_group + member) * LANES
            out_ref[:, column : column + LANES] = hold_ref[
                pl.ds(member, tokens, stride=per_group), :
            ].astype(jnp.bfloat16)


def merge(parts, tokens, kv_heads, per_group):
    rows = tokens * kv_heads * per_group
    spec = pl.BlockSpec(memory_space=VMEM)
    return pl.pallas_call(
        functools.partial(merge_kernel, tokens, kv_heads, per_group, len(parts)),
        out_shape=jax.ShapeDtypeStruct((tokens, kv_heads * per_group * LANES), jnp.bfloat16),
        in_specs=[spec] * len(parts),
        out_specs=spec,
        scratch_shapes=[pltpu.VMEM((tokens * per_group, LANES), jnp.float32)],
        compiler_params=pltpu.CompilerParams(vmem_limit_bytes=8 * 1024 * 1024),
        cost_estimate=pl.CostEstimate(
            flops=4 * len(parts) * rows * LANES,
            bytes_accessed=2 * len(parts) * rows * LANES,
            transcendentals=0,
        ),
        name="merge",
    )(*parts)


def project_kernel(origins, strips, near, columns_from, with_sum, last, *refs):
    count = len(origins)
    blocks, w_refs = refs[:count], refs[count : count + strips]
    rest = refs[count + strips :]
    sum_ref = None
    if with_sum:
        sum_ref, rest = rest[0], rest[1:]
    left_ref = rest[-1]
    n_ctx, n_rep = lax.axis_size("ctx"), lax.axis_size("rep")
    pair, spans = ctx_routes(n_ctx)
    ctx, rep, side = (lax.axis_index(name).astype(jnp.int32) for name in ("ctx", "rep", "heads"))
    group_tokens = left_ref.shape[0]
    for (step, flip, turn), block in zip(origins, blocks):
        tokens = block.shape[0]
        source = lax.rem(lax.div(ctx, pair) + step, spans) * pair + lax.rem(ctx + flip, pair)
        row = (source * n_rep + lax.rem(rep + turn, n_rep)) * tokens
        row = lax.rem(row - side * near + group_tokens, group_tokens)
        start = pl.multiple_of(row, tokens)
        left_ref[pl.ds(start, tokens), :] = block[...]
    depth = left_ref.shape[1]
    width = rest[0].shape[1]
    tile = min(256, width)
    strip = depth // strips
    for start in range(0, width, tile):
        result = None
        for index, w_ref in enumerate(w_refs):
            term = jnp.dot(
                left_ref[:, index * strip : (index + 1) * strip],
                w_ref[:, columns_from + start : columns_from + start + tile],
                preferred_element_type=jnp.float32,
            )
            result = term if result is None else result + term
        if with_sum:
            result = result + sum_ref[:, columns_from + start : columns_from + start + tile]
        if last:
            rest[0][:, start : start + tile] = result[:near]
            rest[1][:, start : start + tile] = result[near:].astype(jnp.bfloat16)
        else:
            rest[0][:, start : start + tile] = result


def project(origins, blocks, weights, partial_sum, near, columns, last):
    depth = blocks[0].shape[1]
    width = columns[1] - columns[0]
    total = sum(block.shape[0] for block in blocks)
    spec = pl.BlockSpec(memory_space=VMEM)
    if last:
        shapes = (
            jax.ShapeDtypeStruct((near, width), jnp.float32),
            jax.ShapeDtypeStruct((total - near, width), jnp.bfloat16),
        )
    else:
        shapes = (jax.ShapeDtypeStruct((total, width), jnp.float32),)
    operands = tuple(blocks) + tuple(weights) + (() if partial_sum is None else (partial_sum,))
    return pl.pallas_call(
        functools.partial(
            project_kernel,
            origins,
            len(weights),
            near,
            columns[0],
            partial_sum is not None,
            last,
        ),
        out_shape=shapes,
        in_specs=[spec] * len(operands),
        out_specs=tuple(spec for _ in shapes),
        scratch_shapes=[pltpu.VMEM((total, depth), jnp.bfloat16)],
        compiler_params=pltpu.CompilerParams(vmem_limit_bytes=8 * 1024 * 1024),
        cost_estimate=pl.CostEstimate(
            flops=2 * total * depth * width,
            bytes_accessed=2 * depth * width,
            transcendentals=0,
        ),
        name="project",
    )(*operands)


def split_index(index, pair):
    return index // pair, index % pair


def ctx_routes(count):
    pair = 2 if count % 2 == 0 else 1
    return pair, count // pair


def moved(value, count, step, flip):
    pair, spans = ctx_routes(count)
    pairs = []
    for source in range(count):
        span, side = split_index(source, pair)
        pairs.append((source, ((span + step) % spans) * pair + (side + flip) % pair))
    return lax.ppermute(value, "ctx", pairs)


def after(value, *others):
    return lax.optimization_barrier((value,) + others)[0]


def gather_keys(count):
    pair, spans = ctx_routes(count)
    crossed = [(step, 0) for step in range(1, spans)]
    near = [(0, 1)] if pair > 1 else []
    far = [(step, 1) for step in range(1, spans)] if pair > 1 else []
    return crossed, near, far


def gather_blocks(value, count):
    crossed, near, far = gather_keys(count)
    blocks = {(0, 0): value}
    for step, flip in crossed:
        blocks[(step, flip)] = moved(value, count, -step, 0)
    for step, flip in near:
        blocks[(step, flip)] = moved(value, count, 0, 1)
    for step, flip in far:
        blocks[(step, flip)] = moved(blocks[(step, 0)], count, 0, 1)
    return blocks


def local(
    queries, cache_keys, cache_values, new_keys, new_values, positions, cached_length, out_weight
):
    tokens, local_heads, size = queries.shape
    block_len, kv_heads = cache_keys.shape[0], cache_keys.shape[1]
    per_group = local_heads // kv_heads
    n_ctx = lax.axis_size("ctx")
    n_rep = lax.axis_size("rep")
    n_heads = lax.axis_size("heads")
    limits = jnp.minimum(cached_length[0], positions)
    marks = jnp.concatenate([limits // 128, limits % 128]).astype(jnp.bfloat16)
    marks = jnp.broadcast_to(marks[:, None], (2 * tokens, size))
    packed = jnp.concatenate([queries.reshape(tokens * local_heads, size), marks], axis=0)

    keys = cache_keys.transpose(1, 0, 2)
    values = cache_values.transpose(1, 0, 2)
    own = (new_keys.transpose(1, 0, 2), new_values.transpose(1, 0, 2))
    chunks = 2 if kv_heads % 2 == 0 else 1
    chunk_heads = kv_heads // chunks
    ranges = [tuple(range(c * chunk_heads, (c + 1) * chunk_heads)) for c in range(chunks)]

    calls = chunks * n_ctx
    strips = max(s for s in range(1, min(calls, 8) + 1) if s % chunks == 0)
    strip = out_weight.shape[0] // strips
    loaded = []

    def run(block, mine):
        found = []
        for heads in ranges:
            index = len(loaded)
            load = (index * strip, (index + 1) * strip) if index < strips else None
            made = attend(
                block,
                keys,
                values,
                own if mine else None,
                out_weight,
                load,
                tokens,
                per_group,
                heads,
            )
            found.append(made[0])
            if load is not None:
                loaded.append(made[1])
        return found

    crossed, close, far = gather_keys(n_ctx)
    visitors = {key: moved(packed, n_ctx, -key[0], 0) for key in crossed}
    visitors.update({key: moved(packed, n_ctx, 0, 1) for key in close})
    parts = [[part] for part in run(packed, True)]
    last = [part[0] for part in parts]
    for key in far:
        visitors[(key[0], 0)] = after(visitors[(key[0], 0)], *last)
        visitors[key] = moved(visitors[(key[0], 0)], n_ctx, 0, 1)
    for key in crossed + close + far:
        block = after(visitors[key], *last)
        last = run(block, False)
        for index, part in enumerate(last):
            parts[index].append(moved(part, n_ctx, key[0], key[1]))

    group_tokens = n_ctx * n_rep * tokens
    near = group_tokens // n_heads
    width = out_weight.shape[1]
    origins = []
    held = []
    for index in range(chunks):
        attended = merge(parts[index], tokens, chunk_heads, per_group)
        blocks = []
        for (step, flip), block in gather_blocks(attended, n_ctx).items():
            for turn in range(n_rep):
                passed = block
                if turn:
                    passed = lax.ppermute(
                        block, "rep", [(i, (i - turn) % n_rep) for i in range(n_rep)]
                    )
                blocks.append(passed)
                if index == 0:
                    origins.append((step, flip, turn))
        held.append(blocks)
    so_far = None
    each = strips // chunks
    for index in range(chunks - 1):
        so_far = project(
            origins, held[index], loaded[index * each : (index + 1) * each], so_far, near, (0, width), False
        )[0]
    pieces = 2 if width % (2 * LANES) == 0 else 1
    results = []
    for piece in range(pieces):
        columns = (piece * width // pieces, (piece + 1) * width // pieces)
        mine, others = project(
            origins, held[-1], loaded[-each:], so_far, near, columns, True
        )
        for step in range(1, n_heads):
            sent = others[(step - 1) * near : step * near]
            mine = mine + lax.ppermute(
                sent, "heads", [(i, (i + step) % n_heads) for i in range(n_heads)]
            ).astype(jnp.float32)
        results.append(mine.astype(jnp.bfloat16))
    return jnp.concatenate(results, axis=1)


def solution(mesh):
    return jax.shard_map(
        local,
        mesh=mesh,
        in_specs=(
            P(("groups", "ctx", "rep"), "heads", None),
            P(("groups", "ctx"), "heads", None),
            P(("groups", "ctx"), "heads", None),
            P(("groups", "ctx", "rep"), "heads", None),
            P(("groups", "ctx", "rep"), "heads", None),
            P(("groups", "ctx", "rep")),
            P("groups"),
            P("heads", ("ctx", "rep")),
        ),
        out_specs=P(("groups", "heads"), ("ctx", "rep")),
        check_vma=False,
    )
```

```python
import functools
import math

import jax
import jax.numpy as jnp
from jax import lax
from jax.experimental import pallas as pl
from jax.experimental.pallas import tpu as pltpu
from jax.sharding import PartitionSpec as P


NEG_FILL = -1e30
NEG_FLOOR = -1e29
LANES = 128
PACK = 16
STREAMS = 4
VMEM = pltpu.MemorySpace.VMEM
SMEM = pltpu.MemorySpace.SMEM
HBM = pltpu.MemorySpace.HBM


def round_up(value, step):
    return (value + step - 1) // step * step


def stat_rows(rows):
    return round_up(3 * (rows // LANES), PACK)


def start_strips(w_ref, strips, strip_refs, sem_ref):
    copies = []
    for index, (strip, strip_ref) in enumerate(zip(strips, strip_refs)):
        rows = strip_ref.shape[0]
        part = rows // STREAMS
        for stream in range(STREAMS):
            copies.append(
                pltpu.make_async_copy(
                    w_ref.at[strip * rows + stream * part : strip * rows + (stream + 1) * part, :],
                    strip_ref.at[stream * part : (stream + 1) * part, :],
                    sem_ref.at[index * STREAMS + stream],
                )
            )
            copies[-1].start()
    return copies


def load_kernel(strips, w_ref, *rest):
    for copy in start_strips(w_ref, strips, rest[:-1], rest[-1]):
        copy.wait()


def load(weight, strips, rows):
    spec = pl.BlockSpec(memory_space=VMEM)
    shape = jax.ShapeDtypeStruct((rows, weight.shape[1]), weight.dtype)
    return pl.pallas_call(
        functools.partial(load_kernel, strips),
        out_shape=[shape] * len(strips),
        in_specs=[pl.BlockSpec(memory_space=HBM)],
        out_specs=[spec] * len(strips),
        scratch_shapes=[pltpu.SemaphoreType.DMA((len(strips) * STREAMS,))],
        compiler_params=pltpu.CompilerParams(vmem_limit_bytes=2 * 1024 * 1024),
        cost_estimate=pl.CostEstimate(
            flops=0, bytes_accessed=len(strips) * rows * weight.shape[1] * 2, transcendentals=0
        ),
        name="load",
    )(pltpu.with_memory_space_constraint(weight, HBM))


def put_levels(out_ref, begin, level):
    first = level.astype(jnp.bfloat16).astype(jnp.float32)
    second = (level - first).astype(jnp.bfloat16).astype(jnp.float32)
    third = level - first - second
    count = level.shape[0]
    extra = stat_rows(count * LANES)
    blank = jnp.zeros((extra - 3 * count, LANES), jnp.float32)
    joined = jnp.concatenate([first, second, third, blank], axis=0)
    out_ref[begin : begin + extra, :] = joined.astype(jnp.bfloat16)


def pack_kernel(positions_ref, length_ref, q_ref, out_ref, mark_ref, sem_ref):
    rows, size = q_ref.shape
    tokens = mark_ref.shape[0] // 2
    copy = pltpu.make_async_copy(q_ref, out_ref.at[:rows, :], sem_ref)
    copy.start()
    for t in range(tokens):
        limit = jnp.minimum(length_ref[0], positions_ref[t])
        high = lax.shift_right_logical(limit, 7).astype(jnp.float32)
        low = lax.bitwise_and(limit, 127).astype(jnp.float32)
        mark_ref[t : t + 1, :] = jnp.full((1, size), high, jnp.float32)
        mark_ref[tokens + t : tokens + t + 1, :] = jnp.full((1, size), low, jnp.float32)
    out_ref[rows:, :] = mark_ref[...].astype(jnp.bfloat16)
    copy.wait()


def pack(queries, positions, length):
    tokens, local_heads, size = queries.shape
    rows = tokens * local_heads
    return pl.pallas_call(
        pack_kernel,
        out_shape=jax.ShapeDtypeStruct((rows + 2 * tokens, size), jnp.bfloat16),
        in_specs=[pl.BlockSpec(memory_space=SMEM)] * 2 + [pl.BlockSpec(memory_space=HBM)],
        out_specs=pl.BlockSpec(memory_space=VMEM),
        scratch_shapes=[pltpu.VMEM((2 * tokens, size), jnp.float32), pltpu.SemaphoreType.DMA],
        compiler_params=pltpu.CompilerParams(vmem_limit_bytes=4 * 1024 * 1024),
        name="pack",
    )(positions, length, pltpu.with_memory_space_constraint(queries.reshape(rows, size), HBM))


def attend_kernel(
    tokens, keep, per_group, with_own, with_prev, strips, q_ref, k_ref, v_ref, *rest
):
    rest = list(rest)
    side = lax.rem(lax.axis_index("ctx").astype(jnp.int32), 2)
    if with_own:
        nk_ref, nv_ref = rest.pop(0), rest.pop(0)
    if with_prev:
        prev_ref = rest.pop(0)
    if strips:
        w_ref = rest.pop(0)
    out_ref = rest.pop(0)
    strip_refs = [rest.pop(0) for _ in strips]
    bound_ref = rest.pop(0)
    copies = start_strips(w_ref, strips, strip_refs, rest.pop(0)) if strips else []
    head_rows = tokens * per_group
    kv_heads, block_len, size = k_ref.shape
    half = kv_heads // 2
    origin = (side if keep else 1 - side) * half
    rows = half * head_rows
    begin = 0
    if with_prev:
        begin = prev_ref.shape[0]
        out_ref[:begin, :] = prev_ref[...]
    local_heads = (q_ref.shape[0] - 2 * tokens) // tokens
    factor = size ** (-0.5) * math.log2(math.e)
    high = q_ref[tokens * local_heads : tokens * local_heads + tokens, :].astype(jnp.float32)
    low = q_ref[tokens * local_heads + tokens :, :].astype(jnp.float32)
    base = lax.axis_index("ctx").astype(jnp.int32) * block_len
    bound = high * 128.0 + low - base.astype(jnp.float32)
    bound_ref[...] = jnp.broadcast_to(bound[:, None, :], (tokens, per_group, LANES)).reshape(
        head_rows, LANES
    )
    lane = lax.broadcasted_iota(jnp.int32, (1, LANES), 1).astype(jnp.float32)
    lane_id = lax.broadcasted_iota(jnp.int32, (LANES, LANES), 1)
    stats = jnp.zeros((LANES, LANES), jnp.float32)
    limit = bound_ref[...]
    for order in range(half):
        head = origin + order
        q = jnp.concatenate(
            [
                q_ref[
                    pl.ds(
                        pl.multiple_of(t * local_heads + head * per_group, per_group), per_group
                    ),
                    :,
                ]
                for t in range(tokens)
            ],
            axis=0,
        )
        scores = lax.dot_general(
            q, k_ref[head], (((1,), (1,)), ((), ())), preferred_element_type=jnp.float32
        )
        pieces = []
        for start in range(0, block_len, LANES):
            seen = (lane + float(start)) < limit
            pieces.append(jnp.where(seen, scores[:, start : start + LANES], NEG_FILL))
        best = functools.reduce(jnp.maximum, pieces)
        top = jnp.max(best, axis=-1, keepdims=True)
        if with_own:
            nk = jnp.broadcast_to(
                nk_ref[head].astype(jnp.float32)[:, None, :], (tokens, per_group, size)
            ).reshape(head_rows, size)
            own = jnp.sum(q.astype(jnp.float32) * nk, axis=-1, keepdims=True)
            top = jnp.maximum(top, own)
        top = jnp.maximum(top, NEG_FLOOR)
        weights = [jnp.exp2((piece - top) * factor) for piece in pieces]
        total = jnp.sum(functools.reduce(jnp.add, weights), axis=-1, keepdims=True)
        rounded = jnp.concatenate([w.astype(jnp.bfloat16) for w in weights], axis=1)
        value = lax.dot_general(
            rounded, v_ref[head], (((1,), (0,)), ((), ())), preferred_element_type=jnp.float32
        )
        if with_own:
            nv = jnp.broadcast_to(
                nv_ref[head].astype(jnp.float32)[:, None, :], (tokens, per_group, size)
            ).reshape(head_rows, size)
            mine = jnp.exp2((own - top) * factor)
            total = total + mine
            value = value + mine * nv
        some = total > 0.0
        safe = jnp.where(some, total, 1.0)
        start = begin + order * head_rows
        out_ref[start : start + head_rows, :] = (value / safe).astype(jnp.bfloat16)
        level = jnp.where(some, top * factor + jnp.log2(safe), NEG_FILL)
        for part in range(head_rows // LANES):
            column = level[part * LANES : (part + 1) * LANES, :]
            index = order * (head_rows // LANES) + part
            stats = jnp.where(lane_id == index, column, stats)
    count = rows // LANES
    put_levels(out_ref, begin + rows, jnp.transpose(stats)[:count])
    for copy in copies:
        copy.wait()


def attend(packed, keep, keys, values, own, prev, weight, strips, rows_each, tokens, per_group):
    kv_heads, block_len, size = keys.shape
    rows = tokens * (kv_heads // 2) * per_group
    body = functools.partial(
        attend_kernel, tokens, keep, per_group, own is not None, prev is not None, strips
    )
    spec = pl.BlockSpec(memory_space=VMEM)
    operands = (packed, keys, values) + (own if own is not None else ())
    length = rows + stat_rows(rows)
    if prev is not None:
        operands += (prev,)
        length += prev.shape[0]
    in_specs = [spec] * len(operands)
    shapes = [jax.ShapeDtypeStruct((length, size), jnp.bfloat16)]
    scratch = [pltpu.VMEM((tokens * per_group, LANES), jnp.float32)]
    if strips:
        operands += (pltpu.with_memory_space_constraint(weight, HBM),)
        in_specs.append(pl.BlockSpec(memory_space=HBM))
        shapes += [jax.ShapeDtypeStruct((rows_each, weight.shape[1]), weight.dtype)] * len(strips)
        scratch.append(pltpu.SemaphoreType.DMA((len(strips) * STREAMS,)))
    return pl.pallas_call(
        body,
        out_shape=shapes,
        in_specs=in_specs,
        out_specs=[spec] * len(shapes),
        scratch_shapes=scratch,
        compiler_params=pltpu.CompilerParams(vmem_limit_bytes=12 * 1024 * 1024),
        cost_estimate=pl.CostEstimate(
            flops=4 * rows * block_len * size,
            bytes_accessed=2 * kv_heads * block_len * size,
            transcendentals=rows * block_len,
        ),
        name="attend",
    )(*operands)


def block_rows(heads, head_rows):
    return heads * head_rows + stat_rows(heads * head_rows)


def blend(refs, sources, heads, head_rows):
    lines = heads * head_rows // LANES
    levels = []
    for index, block, total, first in sources:
        base = block * block_rows(total, head_rows) + total * head_rows
        every = total * head_rows // LANES
        tail = refs[index][base : base + stat_rows(total * head_rows), :].astype(jnp.float32)
        level = tail[:every] + tail[every : 2 * every] + tail[2 * every : 3 * every]
        levels.append(level[first * head_rows // LANES : first * head_rows // LANES + lines])
    top = functools.reduce(jnp.maximum, levels)
    shares = [jnp.exp2(level - top) for level in levels]
    whole = functools.reduce(jnp.add, shares)
    shares = [share / whole for share in shares]
    blank = jnp.zeros((LANES - len(sources) * lines, LANES), jnp.float32)
    columns = jnp.transpose(jnp.concatenate(shares + [blank], axis=0))
    values = []
    for line in range(lines):
        value = None
        for order, (index, block, total, first) in enumerate(sources):
            start = block * block_rows(total, head_rows) + first * head_rows + line * LANES
            share = columns[:, order * lines + line : order * lines + line + 1]
            term = share * refs[index][start : start + LANES, :].astype(jnp.float32)
            value = term if value is None else value + term
        values.append(value)
    return values, top + jnp.log2(whole)


def combine_kernel(count, plan, head_rows, *refs):
    for out_ref, (heads, blocks) in zip(refs[count:], plan):
        begin = 0
        for sources in blocks:
            values, level = blend(refs, sources, heads, head_rows)
            for line, value in enumerate(values):
                start = begin + line * LANES
                out_ref[start : start + LANES, :] = value.astype(jnp.bfloat16)
            put_levels(out_ref, begin + heads * head_rows, level)
            begin += block_rows(heads, head_rows)


def combine(arrays, plan, head_rows):
    spec = pl.BlockSpec(memory_space=VMEM)
    size = arrays[0].shape[1]
    shapes = [
        jax.ShapeDtypeStruct((len(blocks) * block_rows(heads, head_rows), size), jnp.bfloat16)
        for heads, blocks in plan
    ]
    return pl.pallas_call(
        functools.partial(combine_kernel, len(arrays), plan, head_rows),
        out_shape=shapes,
        in_specs=[spec] * len(arrays),
        out_specs=[spec] * len(shapes),
        compiler_params=pltpu.CompilerParams(vmem_limit_bytes=8 * 1024 * 1024),
        cost_estimate=pl.CostEstimate(
            flops=4 * sum(array.size for array in arrays),
            bytes_accessed=2 * sum(array.size for array in arrays),
            transcendentals=0,
        ),
        name="combine",
    )(*arrays)


def merge_kernel(count, plan, tokens, per_group, *refs):
    out_ref, hold_ref = refs[count], refs[count + 1]
    head_rows = tokens * per_group
    for block, column, heads, sources in plan:
        values, _ = blend(refs, sources, heads, head_rows)
        for line, value in enumerate(values):
            hold_ref[line * LANES : (line + 1) * LANES, :] = value
        for member in range(heads * per_group):
            start = (column * per_group + member) * LANES
            row = member // per_group * head_rows + member % per_group
            out_ref[block * tokens : (block + 1) * tokens, start : start + LANES] = hold_ref[
                pl.ds(row, tokens, stride=per_group), :
            ].astype(jnp.bfloat16)


def merge(arrays, plan, tokens, heads, per_group):
    spec = pl.BlockSpec(memory_space=VMEM)
    return pl.pallas_call(
        functools.partial(merge_kernel, len(arrays), plan, tokens, per_group),
        out_shape=jax.ShapeDtypeStruct((2 * tokens, heads * per_group * LANES), jnp.bfloat16),
        in_specs=[spec] * len(arrays),
        out_specs=spec,
        scratch_shapes=[pltpu.VMEM((heads * tokens * per_group, LANES), jnp.float32)],
        compiler_params=pltpu.CompilerParams(vmem_limit_bytes=8 * 1024 * 1024),
        cost_estimate=pl.CostEstimate(
            flops=4 * sum(array.size for array in arrays),
            bytes_accessed=2 * sum(array.size for array in arrays),
            transcendentals=0,
        ),
        name="merge",
    )(*arrays)


def project_kernel(origins, tokens, strips, near, columns_from, with_sum, last, *refs):
    count = len(origins)
    blocks, w_refs = refs[:count], refs[count : count + strips]
    rest = refs[count + strips :]
    sum_ref = None
    if with_sum:
        sum_ref, rest = rest[0], rest[1:]
    left_ref = rest[-1]
    n_ctx, n_rep = lax.axis_size("ctx"), lax.axis_size("rep")
    spans = n_ctx // 2
    ctx, rep, side = (lax.axis_index(name).astype(jnp.int32) for name in ("ctx", "rep", "heads"))
    group_tokens, depth = left_ref.shape
    for (step, flip, turn, offset), block in zip(origins, blocks):
        column = pl.multiple_of(lax.rem(ctx + flip, 2) * (depth // 2), LANES)
        for order in range(2):
            source = lax.rem(lax.div(ctx, 2) + step, spans) * 2 + lax.rem(ctx + flip + order, 2)
            row = (source * n_rep + lax.rem(rep + turn, n_rep)) * tokens
            row = lax.rem(row - side * near + group_tokens, group_tokens)
            left_ref[pl.ds(pl.multiple_of(row, tokens), tokens), pl.ds(column, depth // 2)] = block[
                order * tokens : (order + 1) * tokens, offset : offset + depth // 2
            ]
    width = rest[0].shape[1]
    tile = min(256, width)
    strip = depth // strips
    for start in range(0, width, tile):
        result = None
        for index, w_ref in enumerate(w_refs):
            term = jnp.dot(
                left_ref[:, index * strip : (index + 1) * strip],
                w_ref[:, columns_from + start : columns_from + start + tile],
                preferred_element_type=jnp.float32,
            )
            result = term if result is None else result + term
        if with_sum:
            result = result + sum_ref[:, columns_from + start : columns_from + start + tile]
        if last:
            rest[0][:, start : start + tile] = result[:near]
            rest[1][:, start : start + tile] = result[near:].astype(jnp.bfloat16)
        else:
            rest[0][:, start : start + tile] = result


def project(origins, blocks, weights, partial_sum, tokens, total, near, columns, last):
    depth = sum(weight.shape[0] for weight in weights)
    width = columns[1] - columns[0]
    spec = pl.BlockSpec(memory_space=VMEM)
    if last:
        shapes = (
            jax.ShapeDtypeStruct((near, width), jnp.float32),
            jax.ShapeDtypeStruct((total - near, width), jnp.bfloat16),
        )
    else:
        shapes = (jax.ShapeDtypeStruct((total, width), jnp.float32),)
    operands = tuple(blocks) + tuple(weights) + (() if partial_sum is None else (partial_sum,))
    return pl.pallas_call(
        functools.partial(
            project_kernel,
            tuple(origins),
            tokens,
            len(weights),
            near,
            columns[0],
            partial_sum is not None,
            last,
        ),
        out_shape=shapes,
        in_specs=[spec] * len(operands),
        out_specs=tuple(spec for _ in shapes),
        scratch_shapes=[pltpu.VMEM((total, depth), jnp.bfloat16)],
        compiler_params=pltpu.CompilerParams(vmem_limit_bytes=8 * 1024 * 1024),
        cost_estimate=pl.CostEstimate(
            flops=2 * total * depth * width,
            bytes_accessed=2 * depth * width,
            transcendentals=0,
        ),
        name="project",
    )(*operands)


def after(value, *others):
    return lax.optimization_barrier((value,) + others)[0]


def moved(value, count, step, flip):
    spans = count // 2
    pairs = [
        (i, ((i // 2 + step) % spans) * 2 + (i % 2 + flip) % 2) for i in range(count)
    ]
    return lax.ppermute(value, "ctx", pairs)


def local(
    queries, cache_keys, cache_values, new_keys, new_values, positions, cached_length, out_weight
):
    tokens, local_heads, size = queries.shape
    kv_heads = cache_keys.shape[1]
    per_group = local_heads // kv_heads
    head_rows = tokens * per_group
    n_ctx = lax.axis_size("ctx")
    n_rep = lax.axis_size("rep")
    n_heads = lax.axis_size("heads")
    spans = n_ctx // 2
    half = kv_heads // 2
    units = 2 if half % 2 == 0 else 1
    per_unit = half // units

    packed = pack(queries, positions, cached_length)
    keys = cache_keys.transpose(1, 0, 2)
    values = cache_values.transpose(1, 0, 2)
    own = (new_keys.transpose(1, 0, 2), new_values.transpose(1, 0, 2))

    strips = 2 * kv_heads
    rows_each = out_weight.shape[0] // strips

    def strips_of(unit):
        found = []
        for owner in range(2):
            for head in range(unit * per_unit, (unit + 1) * per_unit):
                found += [2 * (owner * half + head), 2 * (owner * half + head) + 1]
        return found

    pending = [strip for unit in range(units) for strip in strips_of(unit)]
    in_attend = strips // 2
    loaded = {}

    def run(block, keep, mine=False, busy=True, prev=None):
        take = 0 if mine or busy or len(loaded) >= in_attend else 1
        wanted = tuple(pending.pop(0) for _ in range(take))
        made = attend(
            block,
            keep,
            keys,
            values,
            own if mine else None,
            prev,
            out_weight,
            wanted,
            rows_each,
            tokens,
            per_group,
        )
        loaded.update(zip(wanted, made[1:]))
        return made[0]

    near_q = moved(packed, n_ctx, 0, 1)
    cross_q = {j: moved(packed, n_ctx, -j, 0) for j in range(1, spans)}
    own_send = run(packed, False, mine=True)
    back_own = moved(own_send, n_ctx, 0, 1)
    own_keep = run(after(packed, own_send), True, mine=True)
    near_q = after(near_q, own_keep)
    pair_a = run(near_q, False)
    back_a = moved(pair_a, n_ctx, 0, 1)
    far_q = {}
    for j in range(1, spans):
        cross_q[j] = after(cross_q[j], pair_a)
        far_q[j] = moved(cross_q[j], n_ctx, 0, 1)
    p_keep = run(after(near_q, pair_a), True, busy=False)

    def source(index, block, total, first):
        return (index, block, total, first)

    def both(heads, unit):
        first = unit * heads
        return (
            (source(0, 0, half, first), source(2, 0, half, first)),
            (source(1, 0, half, first), source(3, 0, half, first)),
        )

    chunks = {}
    last = p_keep
    done_a = False
    for j in range(1, spans):
        c_send = run(after(cross_q[j], last), False, busy=False)
        back_c = moved(c_send, n_ctx, 0, 1)
        last = c_send
        if not done_a:
            done_a = True
            (made,) = combine(
                (own_keep, p_keep, after(back_a, last), back_own),
                ((half, both(half, 0)),),
                head_rows,
            )
            chunks[0] = [(made, half, unit * per_unit) for unit in range(units)]
            got_a = {s: moved(made, n_ctx, s, 0) for s in range(1, spans)}
            last = made
        block_f = after(far_q[j], last)
        pair_b = run(block_f, False)
        back_b = moved(pair_b, n_ctx, 0, 1)
        c_keep = run(after(cross_q[j], pair_b), True, busy=False)
        f_keep = run(after(block_f, c_keep), True, busy=False)
        made = combine(
            (c_keep, f_keep, after(back_b, f_keep), back_c),
            tuple((per_unit, both(per_unit, unit)) for unit in range(units)),
            head_rows,
        )
        chunks[j] = [(piece, per_unit, 0) for piece in made]
        last = made[0]
    if not done_a:
        (made,) = combine((own_keep, p_keep, back_a, back_own), ((half, both(half, 0)),), head_rows)
        chunks[0] = [(made, half, unit * per_unit) for unit in range(units)]
        got_a = {}
        last = made
    got = {}
    for s in range(1, spans):
        got[s, 0] = [(got_a[s], half, unit * per_unit) for unit in range(units)]
        for j in range(1, spans):
            got[s, j] = [
                (moved(piece, n_ctx, s, 0), total, first)
                for piece, total, first in chunks[j]
            ]

    def fetch(count, gate):
        wanted = tuple(pending.pop(0) for _ in range(min(count, len(pending))))
        if wanted:
            made = load(after(out_weight, gate), wanted, rows_each)
            loaded.update(zip(wanted, made))

    def merged(j, wanted):
        arrays, plan = [], []
        for column, unit in enumerate(wanted):
            for block in range(2):
                picked = []
                for piece, total, first in [chunks[j][unit]] + [
                    got[s, (j + s) % spans][unit] for s in range(1, spans)
                ]:
                    index = next((i for i, seen in enumerate(arrays) if seen is piece), len(arrays))
                    if index == len(arrays):
                        arrays.append(piece)
                    picked.append(source(index, block, total, first))
                plan.append((block, column * per_unit, per_unit, tuple(picked)))
        return merge(tuple(arrays), tuple(plan), tokens, per_unit * len(wanted), per_group)

    def spread(array):
        entries = []
        for flip, block in ((0, array), (1, moved(array, n_ctx, 0, 1))):
            for turn in range(n_rep):
                passed = block
                if turn:
                    passed = lax.ppermute(
                        block, "rep", [(i, (i - turn) % n_rep) for i in range(n_rep)]
                    )
                entries.append((flip, turn, passed))
        return entries

    depth = per_unit * per_group * size
    held = [[] for _ in range(units)]
    fetch(len(pending) // 2, last)
    for j in range(1, spans):
        array = merged(j, range(units))
        for flip, turn, passed in spread(array):
            for unit in range(units):
                held[unit].append(((j, flip, turn, unit * depth), passed))
    for unit in range(units):
        array = merged(0, (unit,))
        if unit == 0:
            fetch(len(pending), array)
        for flip, turn, passed in spread(array):
            held[unit].append(((0, flip, turn, 0), passed))

    total = n_ctx * n_rep * tokens
    near = total // n_heads
    width = out_weight.shape[1]
    so_far = None
    for unit in range(units - 1):
        so_far = project(
            [entry[0] for entry in held[unit]],
            [entry[1] for entry in held[unit]],
            [loaded[strip] for strip in strips_of(unit)],
            so_far,
            tokens,
            total,
            near,
            (0, width),
            False,
        )[0]
    pieces = 2 if width % (2 * LANES) == 0 else 1
    results = []
    for piece in range(pieces):
        columns = (piece * width // pieces, (piece + 1) * width // pieces)
        mine, others = project(
            [entry[0] for entry in held[-1]],
            [entry[1] for entry in held[-1]],
            [loaded[strip] for strip in strips_of(units - 1)],
            so_far,
            tokens,
            total,
            near,
            columns,
            True,
        )
        for step in range(1, n_heads):
            sent = others[(step - 1) * near : step * near]
            mine = mine + lax.ppermute(
                sent, "heads", [(i, (i + step) % n_heads) for i in range(n_heads)]
            ).astype(jnp.float32)
        results.append(mine.astype(jnp.bfloat16))
    return jnp.concatenate(results, axis=1)


def solution(mesh):
    return jax.shard_map(
        local,
        mesh=mesh,
        in_specs=(
            P(("groups", "ctx", "rep"), "heads", None),
            P(("groups", "ctx"), "heads", None),
            P(("groups", "ctx"), "heads", None),
            P(("groups", "ctx", "rep"), "heads", None),
            P(("groups", "ctx", "rep"), "heads", None),
            P(("groups", "ctx", "rep")),
            P("groups"),
            P("heads", ("ctx", "rep")),
        ),
        out_specs=P(("groups", "heads"), ("ctx", "rep")),
        check_vma=False,
    )
```

```python
import functools
import math

import jax
import jax.numpy as jnp
from jax import lax
from jax.experimental import pallas as pl
from jax.experimental.pallas import tpu as pltpu
from jax.sharding import PartitionSpec as P


NEG_FILL = -1e30
NEG_FLOOR = -1e29
LANES = 128
PACK = 16
STREAMS = 4
VMEM = pltpu.MemorySpace.VMEM
SMEM = pltpu.MemorySpace.SMEM
HBM = pltpu.MemorySpace.HBM


def round_up(value, step):
    return (value + step - 1) // step * step


def stat_rows(rows):
    return round_up(3 * (rows // LANES), PACK)


def start_strips(w_ref, strips, strip_refs, sem_ref):
    copies = []
    for index, (strip, strip_ref) in enumerate(zip(strips, strip_refs)):
        rows = strip_ref.shape[0]
        part = rows // STREAMS
        for stream in range(STREAMS):
            copies.append(
                pltpu.make_async_copy(
                    w_ref.at[strip * rows + stream * part : strip * rows + (stream + 1) * part, :],
                    strip_ref.at[stream * part : (stream + 1) * part, :],
                    sem_ref.at[index * STREAMS + stream],
                )
            )
            copies[-1].start()
    return copies


def load_kernel(strips, w_ref, *rest):
    for copy in start_strips(w_ref, strips, rest[:-1], rest[-1]):
        copy.wait()


def load(weight, strips, rows):
    spec = pl.BlockSpec(memory_space=VMEM)
    shape = jax.ShapeDtypeStruct((rows, weight.shape[1]), weight.dtype)
    return pl.pallas_call(
        functools.partial(load_kernel, strips),
        out_shape=[shape] * len(strips),
        in_specs=[pl.BlockSpec(memory_space=HBM)],
        out_specs=[spec] * len(strips),
        scratch_shapes=[pltpu.SemaphoreType.DMA((len(strips) * STREAMS,))],
        compiler_params=pltpu.CompilerParams(vmem_limit_bytes=2 * 1024 * 1024),
        cost_estimate=pl.CostEstimate(
            flops=0, bytes_accessed=len(strips) * rows * weight.shape[1] * 2, transcendentals=0
        ),
        name="load",
    )(pltpu.with_memory_space_constraint(weight, HBM))


def put_levels(out_ref, begin, level):
    first = level.astype(jnp.bfloat16).astype(jnp.float32)
    second = (level - first).astype(jnp.bfloat16).astype(jnp.float32)
    third = level - first - second
    count = level.shape[0]
    extra = stat_rows(count * LANES)
    blank = jnp.zeros((extra - 3 * count, LANES), jnp.float32)
    joined = jnp.concatenate([first, second, third, blank], axis=0)
    out_ref[begin : begin + extra, :] = joined.astype(jnp.bfloat16)


def pack_kernel(positions_ref, length_ref, q_ref, out_ref, mark_ref, sem_ref):
    rows, size = q_ref.shape
    tokens = mark_ref.shape[0] // 2
    copy = pltpu.make_async_copy(q_ref, out_ref.at[:rows, :], sem_ref)
    copy.start()
    for t in range(tokens):
        limit = jnp.minimum(length_ref[0], positions_ref[t])
        high = lax.shift_right_logical(limit, 7).astype(jnp.float32)
        low = lax.bitwise_and(limit, 127).astype(jnp.float32)
        mark_ref[t : t + 1, :] = jnp.full((1, size), high, jnp.float32)
        mark_ref[tokens + t : tokens + t + 1, :] = jnp.full((1, size), low, jnp.float32)
    out_ref[rows:, :] = mark_ref[...].astype(jnp.bfloat16)
    copy.wait()


def pack(queries, positions, length):
    tokens, local_heads, size = queries.shape
    rows = tokens * local_heads
    return pl.pallas_call(
        pack_kernel,
        out_shape=jax.ShapeDtypeStruct((rows + 2 * tokens, size), jnp.bfloat16),
        in_specs=[pl.BlockSpec(memory_space=SMEM)] * 2 + [pl.BlockSpec(memory_space=HBM)],
        out_specs=pl.BlockSpec(memory_space=VMEM),
        scratch_shapes=[pltpu.VMEM((2 * tokens, size), jnp.float32), pltpu.SemaphoreType.DMA],
        compiler_params=pltpu.CompilerParams(vmem_limit_bytes=4 * 1024 * 1024),
        name="pack",
    )(positions, length, pltpu.with_memory_space_constraint(queries.reshape(rows, size), HBM))


def attend_kernel(
    tokens, keep, per_group, with_own, with_prev, strips, q_ref, k_ref, v_ref, *rest
):
    rest = list(rest)
    side = lax.rem(lax.axis_index("ctx").astype(jnp.int32), 2)
    if with_own:
        nk_ref, nv_ref = rest.pop(0), rest.pop(0)
    if with_prev:
        prev_ref = rest.pop(0)
    if strips:
        w_ref = rest.pop(0)
    out_ref = rest.pop(0)
    strip_refs = [rest.pop(0) for _ in strips]
    bound_ref = rest.pop(0)
    copies = start_strips(w_ref, strips, strip_refs, rest.pop(0)) if strips else []
    head_rows = tokens * per_group
    kv_heads, block_len, size = k_ref.shape
    half = kv_heads // 2
    origin = (side if keep else 1 - side) * half
    rows = half * head_rows
    begin = 0
    if with_prev:
        begin = prev_ref.shape[0]
        out_ref[:begin, :] = prev_ref[...]
    local_heads = (q_ref.shape[0] - 2 * tokens) // tokens
    factor = size ** (-0.5) * math.log2(math.e)
    high = q_ref[tokens * local_heads : tokens * local_heads + tokens, :].astype(jnp.float32)
    low = q_ref[tokens * local_heads + tokens :, :].astype(jnp.float32)
    base = lax.axis_index("ctx").astype(jnp.int32) * block_len
    bound = high * 128.0 + low - base.astype(jnp.float32)
    bound_ref[...] = jnp.broadcast_to(bound[:, None, :], (tokens, per_group, LANES)).reshape(
        head_rows, LANES
    )
    lane = lax.broadcasted_iota(jnp.int32, (1, LANES), 1).astype(jnp.float32)
    lane_id = lax.broadcasted_iota(jnp.int32, (LANES, LANES), 1)
    stats = jnp.zeros((LANES, LANES), jnp.float32)
    limit = bound_ref[...]
    for order in range(half):
        head = origin + order
        q = jnp.concatenate(
            [
                q_ref[
                    pl.ds(
                        pl.multiple_of(t * local_heads + head * per_group, per_group), per_group
                    ),
                    :,
                ]
                for t in range(tokens)
            ],
            axis=0,
        )
        scores = lax.dot_general(
            q, k_ref[head], (((1,), (1,)), ((), ())), preferred_element_type=jnp.float32
        )
        pieces = []
        for start in range(0, block_len, LANES):
            seen = (lane + float(start)) < limit
            pieces.append(jnp.where(seen, scores[:, start : start + LANES], NEG_FILL))
        best = functools.reduce(jnp.maximum, pieces)
        top = jnp.max(best, axis=-1, keepdims=True)
        if with_own:
            nk = jnp.broadcast_to(
                nk_ref[head].astype(jnp.float32)[:, None, :], (tokens, per_group, size)
            ).reshape(head_rows, size)
            own = jnp.sum(q.astype(jnp.float32) * nk, axis=-1, keepdims=True)
            top = jnp.maximum(top, own)
        top = jnp.maximum(top, NEG_FLOOR)
        weights = [jnp.exp2((piece - top) * factor) for piece in pieces]
        total = jnp.sum(functools.reduce(jnp.add, weights), axis=-1, keepdims=True)
        rounded = jnp.concatenate([w.astype(jnp.bfloat16) for w in weights], axis=1)
        value = lax.dot_general(
            rounded, v_ref[head], (((1,), (0,)), ((), ())), preferred_element_type=jnp.float32
        )
        if with_own:
            nv = jnp.broadcast_to(
                nv_ref[head].astype(jnp.float32)[:, None, :], (tokens, per_group, size)
            ).reshape(head_rows, size)
            mine = jnp.exp2((own - top) * factor)
            total = total + mine
            value = value + mine * nv
        some = total > 0.0
        safe = jnp.where(some, total, 1.0)
        start = begin + order * head_rows
        out_ref[start : start + head_rows, :] = (value / safe).astype(jnp.bfloat16)
        level = jnp.where(some, top * factor + jnp.log2(safe), NEG_FILL)
        for part in range(head_rows // LANES):
            column = level[part * LANES : (part + 1) * LANES, :]
            index = order * (head_rows // LANES) + part
            stats = jnp.where(lane_id == index, column, stats)
    count = rows // LANES
    put_levels(out_ref, begin + rows, jnp.transpose(stats)[:count])
    for copy in copies:
        copy.wait()


def attend(packed, keep, keys, values, own, prev, weight, strips, rows_each, tokens, per_group):
    kv_heads, block_len, size = keys.shape
    rows = tokens * (kv_heads // 2) * per_group
    body = functools.partial(
        attend_kernel, tokens, keep, per_group, own is not None, prev is not None, strips
    )
    spec = pl.BlockSpec(memory_space=VMEM)
    operands = (packed, keys, values) + (own if own is not None else ())
    length = rows + stat_rows(rows)
    if prev is not None:
        operands += (prev,)
        length += prev.shape[0]
    in_specs = [spec] * len(operands)
    shapes = [jax.ShapeDtypeStruct((length, size), jnp.bfloat16)]
    scratch = [pltpu.VMEM((tokens * per_group, LANES), jnp.float32)]
    if strips:
        operands += (pltpu.with_memory_space_constraint(weight, HBM),)
        in_specs.append(pl.BlockSpec(memory_space=HBM))
        shapes += [jax.ShapeDtypeStruct((rows_each, weight.shape[1]), weight.dtype)] * len(strips)
        scratch.append(pltpu.SemaphoreType.DMA((len(strips) * STREAMS,)))
    return pl.pallas_call(
        body,
        out_shape=shapes,
        in_specs=in_specs,
        out_specs=[spec] * len(shapes),
        scratch_shapes=scratch,
        compiler_params=pltpu.CompilerParams(vmem_limit_bytes=12 * 1024 * 1024),
        cost_estimate=pl.CostEstimate(
            flops=4 * rows * block_len * size,
            bytes_accessed=2 * kv_heads * block_len * size,
            transcendentals=rows * block_len,
        ),
        name="attend",
    )(*operands)


def block_rows(heads, head_rows):
    return heads * head_rows + stat_rows(heads * head_rows)


def blend(refs, sources, heads, head_rows):
    lines = heads * head_rows // LANES
    levels = []
    for index, block, total, first in sources:
        base = block * block_rows(total, head_rows) + total * head_rows
        every = total * head_rows // LANES
        tail = refs[index][base : base + stat_rows(total * head_rows), :].astype(jnp.float32)
        level = tail[:every] + tail[every : 2 * every] + tail[2 * every : 3 * every]
        levels.append(level[first * head_rows // LANES : first * head_rows // LANES + lines])
    top = functools.reduce(jnp.maximum, levels)
    shares = [jnp.exp2(level - top) for level in levels]
    whole = functools.reduce(jnp.add, shares)
    shares = [share / whole for share in shares]
    blank = jnp.zeros((LANES - len(sources) * lines, LANES), jnp.float32)
    columns = jnp.transpose(jnp.concatenate(shares + [blank], axis=0))
    values = []
    for line in range(lines):
        value = None
        for order, (index, block, total, first) in enumerate(sources):
            start = block * block_rows(total, head_rows) + first * head_rows + line * LANES
            share = columns[:, order * lines + line : order * lines + line + 1]
            term = share * refs[index][start : start + LANES, :].astype(jnp.float32)
            value = term if value is None else value + term
        values.append(value)
    return values, top + jnp.log2(whole)


def combine_kernel(count, plan, head_rows, *refs):
    for out_ref, (heads, blocks) in zip(refs[count:], plan):
        begin = 0
        for sources in blocks:
            values, level = blend(refs, sources, heads, head_rows)
            for line, value in enumerate(values):
                start = begin + line * LANES
                out_ref[start : start + LANES, :] = value.astype(jnp.bfloat16)
            put_levels(out_ref, begin + heads * head_rows, level)
            begin += block_rows(heads, head_rows)


def combine(arrays, plan, head_rows):
    spec = pl.BlockSpec(memory_space=VMEM)
    size = arrays[0].shape[1]
    shapes = [
        jax.ShapeDtypeStruct((len(blocks) * block_rows(heads, head_rows), size), jnp.bfloat16)
        for heads, blocks in plan
    ]
    return pl.pallas_call(
        functools.partial(combine_kernel, len(arrays), plan, head_rows),
        out_shape=shapes,
        in_specs=[spec] * len(arrays),
        out_specs=[spec] * len(shapes),
        compiler_params=pltpu.CompilerParams(vmem_limit_bytes=8 * 1024 * 1024),
        cost_estimate=pl.CostEstimate(
            flops=4 * sum(array.size for array in arrays),
            bytes_accessed=2 * sum(array.size for array in arrays),
            transcendentals=0,
        ),
        name="combine",
    )(*arrays)


def merge_kernel(count, plan, tokens, per_group, *refs):
    out_ref, hold_ref = refs[count], refs[count + 1]
    head_rows = tokens * per_group
    for block, column, heads, sources in plan:
        values, _ = blend(refs, sources, heads, head_rows)
        for line, value in enumerate(values):
            hold_ref[line * LANES : (line + 1) * LANES, :] = value
        for member in range(heads * per_group):
            start = (column * per_group + member) * LANES
            row = member // per_group * head_rows + member % per_group
            out_ref[block * tokens : (block + 1) * tokens, start : start + LANES] = hold_ref[
                pl.ds(row, tokens, stride=per_group), :
            ].astype(jnp.bfloat16)


def merge(arrays, plan, tokens, heads, per_group):
    spec = pl.BlockSpec(memory_space=VMEM)
    return pl.pallas_call(
        functools.partial(merge_kernel, len(arrays), plan, tokens, per_group),
        out_shape=jax.ShapeDtypeStruct((2 * tokens, heads * per_group * LANES), jnp.bfloat16),
        in_specs=[spec] * len(arrays),
        out_specs=spec,
        scratch_shapes=[pltpu.VMEM((heads * tokens * per_group, LANES), jnp.float32)],
        compiler_params=pltpu.CompilerParams(vmem_limit_bytes=8 * 1024 * 1024),
        cost_estimate=pl.CostEstimate(
            flops=4 * sum(array.size for array in arrays),
            bytes_accessed=2 * sum(array.size for array in arrays),
            transcendentals=0,
        ),
        name="merge",
    )(*arrays)


def project_kernel(origins, tokens, strips, near, columns_from, with_sum, last, *refs):
    count = len(origins)
    blocks, w_refs = refs[:count], refs[count : count + strips]
    rest = refs[count + strips :]
    sum_ref = None
    if with_sum:
        sum_ref, rest = rest[0], rest[1:]
    left_ref = rest[-1]
    n_ctx, n_rep = lax.axis_size("ctx"), lax.axis_size("rep")
    spans = n_ctx // 2
    ctx, rep, side = (lax.axis_index(name).astype(jnp.int32) for name in ("ctx", "rep", "heads"))
    group_tokens, depth = left_ref.shape
    for (step, flip, turn, offset), block in zip(origins, blocks):
        column = pl.multiple_of(lax.rem(ctx + flip, 2) * (depth // 2), LANES)
        for order in range(2):
            source = lax.rem(lax.div(ctx, 2) + step, spans) * 2 + lax.rem(ctx + flip + order, 2)
            row = (source * n_rep + lax.rem(rep + turn, n_rep)) * tokens
            row = lax.rem(row - side * near + group_tokens, group_tokens)
            left_ref[pl.ds(pl.multiple_of(row, tokens), tokens), pl.ds(column, depth // 2)] = block[
                order * tokens : (order + 1) * tokens, offset : offset + depth // 2
            ]
    width = rest[0].shape[1]
    tile = min(256, width)
    strip = depth // strips
    for start in range(0, width, tile):
        result = None
        for index, w_ref in enumerate(w_refs):
            term = jnp.dot(
                left_ref[:, index * strip : (index + 1) * strip],
                w_ref[:, columns_from + start : columns_from + start + tile],
                preferred_element_type=jnp.float32,
            )
            result = term if result is None else result + term
        if with_sum:
            result = result + sum_ref[:, columns_from + start : columns_from + start + tile]
        if last:
            rest[0][:, start : start + tile] = result[:near]
            rest[1][:, start : start + tile] = result[near:].astype(jnp.bfloat16)
        else:
            rest[0][:, start : start + tile] = result


def project(origins, blocks, weights, partial_sum, tokens, total, near, columns, last):
    depth = sum(weight.shape[0] for weight in weights)
    width = columns[1] - columns[0]
    spec = pl.BlockSpec(memory_space=VMEM)
    if last:
        shapes = (
            jax.ShapeDtypeStruct((near, width), jnp.float32),
            jax.ShapeDtypeStruct((total - near, width), jnp.bfloat16),
        )
    else:
        shapes = (jax.ShapeDtypeStruct((total, width), jnp.float32),)
    operands = tuple(blocks) + tuple(weights) + (() if partial_sum is None else (partial_sum,))
    return pl.pallas_call(
        functools.partial(
            project_kernel,
            tuple(origins),
            tokens,
            len(weights),
            near,
            columns[0],
            partial_sum is not None,
            last,
        ),
        out_shape=shapes,
        in_specs=[spec] * len(operands),
        out_specs=tuple(spec for _ in shapes),
        scratch_shapes=[pltpu.VMEM((total, depth), jnp.bfloat16)],
        compiler_params=pltpu.CompilerParams(vmem_limit_bytes=8 * 1024 * 1024),
        cost_estimate=pl.CostEstimate(
            flops=2 * total * depth * width,
            bytes_accessed=2 * depth * width,
            transcendentals=0,
        ),
        name="project",
    )(*operands)


def after(value, *others):
    return lax.optimization_barrier((value,) + others)[0]


def moved(value, count, step, flip):
    spans = count // 2
    pairs = [
        (i, ((i // 2 + step) % spans) * 2 + (i % 2 + flip) % 2) for i in range(count)
    ]
    return lax.ppermute(value, "ctx", pairs)


def local(
    queries, cache_keys, cache_values, new_keys, new_values, positions, cached_length, out_weight
):
    tokens, local_heads, size = queries.shape
    kv_heads = cache_keys.shape[1]
    per_group = local_heads // kv_heads
    head_rows = tokens * per_group
    n_ctx = lax.axis_size("ctx")
    n_rep = lax.axis_size("rep")
    n_heads = lax.axis_size("heads")
    spans = n_ctx // 2
    half = kv_heads // 2
    units = 2 if half % 2 == 0 else 1
    per_unit = half // units

    packed = pack(queries, positions, cached_length)
    keys = cache_keys.transpose(1, 0, 2)
    values = cache_values.transpose(1, 0, 2)
    own = (new_keys.transpose(1, 0, 2), new_values.transpose(1, 0, 2))

    strips = 2 * kv_heads
    rows_each = out_weight.shape[0] // strips

    def strips_of(unit):
        found = []
        for owner in range(2):
            for head in range(unit * per_unit, (unit + 1) * per_unit):
                found += [2 * (owner * half + head), 2 * (owner * half + head) + 1]
        return found

    pending = [strip for unit in range(units) for strip in strips_of(unit)]
    in_attend = min(3, strips // 2)
    loaded = {}

    def run(block, keep, mine=False, busy=True, prev=None):
        take = 0 if busy or len(loaded) >= in_attend else 1
        wanted = tuple(pending.pop(0) for _ in range(take))
        made = attend(
            block,
            keep,
            keys,
            values,
            own if mine else None,
            prev,
            out_weight,
            wanted,
            rows_each,
            tokens,
            per_group,
        )
        loaded.update(zip(wanted, made[1:]))
        return made[0]

    near_q = moved(packed, n_ctx, 0, 1)
    cross_q = {j: moved(packed, n_ctx, -j, 0) for j in range(1, spans)}
    own_send = run(packed, False, mine=True)
    back_own = moved(own_send, n_ctx, 0, 1)
    own_keep = run(after(packed, own_send), True, mine=True, busy=False)
    near_q = after(near_q, own_keep)
    pair_a = run(near_q, False)
    back_a = moved(pair_a, n_ctx, 0, 1)
    far_q = {}
    for j in range(1, spans):
        cross_q[j] = after(cross_q[j], pair_a)
        far_q[j] = moved(cross_q[j], n_ctx, 0, 1)
    p_keep = run(after(near_q, pair_a), True)

    def source(index, block, total, first):
        return (index, block, total, first)

    def both(heads, unit):
        first = unit * heads
        return (
            (source(0, 0, half, first), source(2, 0, half, first)),
            (source(1, 0, half, first), source(3, 0, half, first)),
        )

    chunks = {}
    last = p_keep
    done_a = False
    for j in range(1, spans):
        c_send = run(after(cross_q[j], last), False)
        back_c = moved(c_send, n_ctx, 0, 1)
        last = c_send
        if not done_a:
            done_a = True
            (made,) = combine(
                (own_keep, p_keep, after(back_a, last), back_own),
                ((half, both(half, 0)),),
                head_rows,
            )
            chunks[0] = [(made, half, unit * per_unit) for unit in range(units)]
            got_a = {s: moved(made, n_ctx, s, 0) for s in range(1, spans)}
            last = made
        block_f = after(far_q[j], last)
        pair_b = run(block_f, False)
        back_b = moved(pair_b, n_ctx, 0, 1)
        c_keep = run(after(cross_q[j], pair_b), True, busy=False)
        f_keep = run(after(block_f, c_keep), True, busy=False)
        made = combine(
            (c_keep, f_keep, after(back_b, f_keep), back_c),
            tuple((per_unit, both(per_unit, unit)) for unit in range(units)),
            head_rows,
        )
        chunks[j] = [(piece, per_unit, 0) for piece in made]
        last = made[0]
    if not done_a:
        (made,) = combine((own_keep, p_keep, back_a, back_own), ((half, both(half, 0)),), head_rows)
        chunks[0] = [(made, half, unit * per_unit) for unit in range(units)]
        got_a = {}
        last = made
    got = {}
    for s in range(1, spans):
        got[s, 0] = [(got_a[s], half, unit * per_unit) for unit in range(units)]
        for j in range(1, spans):
            got[s, j] = [
                (moved(piece, n_ctx, s, 0), total, first)
                for piece, total, first in chunks[j]
            ]

    def fetch(count, gate):
        wanted = tuple(pending.pop(0) for _ in range(min(count, len(pending))))
        if wanted:
            made = load(after(out_weight, gate), wanted, rows_each)
            loaded.update(zip(wanted, made))

    def merged(j, wanted):
        arrays, plan = [], []
        for column, unit in enumerate(wanted):
            for block in range(2):
                picked = []
                for piece, total, first in [chunks[j][unit]] + [
                    got[s, (j + s) % spans][unit] for s in range(1, spans)
                ]:
                    index = next((i for i, seen in enumerate(arrays) if seen is piece), len(arrays))
                    if index == len(arrays):
                        arrays.append(piece)
                    picked.append(source(index, block, total, first))
                plan.append((block, column * per_unit, per_unit, tuple(picked)))
        return merge(tuple(arrays), tuple(plan), tokens, per_unit * len(wanted), per_group)

    def spread(array):
        entries = []
        for flip, block in ((0, array), (1, moved(array, n_ctx, 0, 1))):
            for turn in range(n_rep):
                passed = block
                if turn:
                    passed = lax.ppermute(
                        block, "rep", [(i, (i - turn) % n_rep) for i in range(n_rep)]
                    )
                entries.append((flip, turn, passed))
        return entries

    depth = per_unit * per_group * size
    held = [[] for _ in range(units)]
    fetch(2 if units > 1 else len(pending), last)
    for j in range(1, spans):
        array = merged(j, range(units))
        for flip, turn, passed in spread(array):
            for unit in range(units):
                held[unit].append(((j, flip, turn, unit * depth), passed))
    for unit in range(units):
        array = merged(0, (unit,))
        if unit == 0:
            fetch(2, array)
        for flip, turn, passed in spread(array):
            held[unit].append(((0, flip, turn, 0), passed))

    total = n_ctx * n_rep * tokens
    near = total // n_heads
    width = out_weight.shape[1]
    so_far = None
    for unit in range(units - 1):
        so_far = project(
            [entry[0] for entry in held[unit]],
            [entry[1] for entry in held[unit]],
            [loaded[strip] for strip in strips_of(unit)],
            so_far,
            tokens,
            total,
            near,
            (0, width),
            False,
        )[0]
        fetch(len(pending), so_far)
    pieces = 2 if width % (2 * LANES) == 0 else 1
    first = width * 3 // 8 // 256 * 256 or width // 2
    edges = (0, first, width) if pieces == 2 else (0, width)
    results = []
    for piece in range(pieces):
        columns = (edges[piece], edges[piece + 1])
        mine, others = project(
            [entry[0] for entry in held[-1]],
            [entry[1] for entry in held[-1]],
            [loaded[strip] for strip in strips_of(units - 1)],
            so_far,
            tokens,
            total,
            near,
            columns,
            True,
        )
        for step in range(1, n_heads):
            sent = others[(step - 1) * near : step * near]
            mine = mine + lax.ppermute(
                sent, "heads", [(i, (i + step) % n_heads) for i in range(n_heads)]
            ).astype(jnp.float32)
        results.append(mine.astype(jnp.bfloat16))
    return jnp.concatenate(results, axis=1)


def solution(mesh):
    return jax.shard_map(
        local,
        mesh=mesh,
        in_specs=(
            P(("groups", "ctx", "rep"), "heads", None),
            P(("groups", "ctx"), "heads", None),
            P(("groups", "ctx"), "heads", None),
            P(("groups", "ctx", "rep"), "heads", None),
            P(("groups", "ctx", "rep"), "heads", None),
            P(("groups", "ctx", "rep")),
            P("groups"),
            P("heads", ("ctx", "rep")),
        ),
        out_specs=P(("groups", "heads"), ("ctx", "rep")),
        check_vma=False,
    )
```
